512 devices in a mesh: lat: 16 (over x, y_hi), lon: 32 (over y_lo, z, core).
Axes of the slice: x: 4, y: 8 (y_hi: 4, y_lo: 2; y = y_hi * 2 + y_lo), z: 8, core: 2. Of those that a mesh axis runs over, the one named last changes fastest.
Arguments:
- queries: bfloat16 [256, 384, 512], P('lat', 'lon'), may hold values from -70 to 70
- keys: bfloat16 [256, 384, 512], P('lat', 'lon'), may hold values from -4.5 to 4.5
- values: bfloat16 [256, 384, 512], P('lat', 'lon'), may hold values from -6 to 6
- out_weight: bfloat16 [512, 512], replicated, may hold values from -0.25 to 0.25
- d_out: bfloat16 [256, 384, 512], P('lat', 'lon'), may hold values from -6 to 6
Outputs:
- d_queries: bfloat16 [256, 384, 512], P('lat', 'lon')
- d_keys: bfloat16 [256, 384, 512], P('lat', 'lon')
- d_values: bfloat16 [256, 384, 512], P('lat', 'lon')
- d_weight: bfloat16 [512, 512], replicated
The draws below stay inside these ranges and needn't reach their ends.
All inputs are finite; a program needn't handle non-finite values.
Results may differ from the reference program's by a relative error of at most 0.0096.
Values may be sent and summed in bfloat16 or wider, within the bound.
A program may use at most 64 MiB of HBM per device.

```python
import jax
import jax.numpy as jnp
from jax import lax

C = 512
HEADS = 8
HEAD = 64
RADIUS = 6
LAT = 256
LON = 384
TOKENS = 98304


def draw_keys(key, part):
    result = jnp.clip(jax.random.normal(jax.random.fold_in(key, 21), (LAT, LON, C), jnp.float32), -4.5, 4.5)
    return result.astype(jnp.bfloat16)


def draw_queries(key, part):
    result = jnp.clip(jax.random.normal(jax.random.fold_in(key, 22), (LAT, LON, C), jnp.float32), -4.5, 4.5)
    return result.astype(jnp.bfloat16)


def block_scale(rng, extent, shards, low, top_value):
    def one(position, parts):
        steps = jax.random.uniform(jax.random.fold_in(jax.random.fold_in(rng, 6), position), (parts,), jnp.float32, low / len(shards), top_value / len(shards))
        return jnp.repeat(jnp.exp(steps), extent[position] // parts).reshape((-1,) + (1,) * (len(extent) - position - 1))

    loudness = one(*shards[0])
    for cut in shards[1:]:
        loudness = loudness * one(*cut)
    return loudness


def gaussian(rng, extent, width, limit, shards=(), held_as=jnp.bfloat16):
    drawn = width * jax.random.normal(rng, extent, jnp.float32)
    if shards:
        drawn = drawn * block_scale(rng, extent, shards, -0.22, 0.18)
    return jnp.clip(drawn, -limit, limit).astype(held_as)


def setup_inputs(seed: int = 0) -> dict:
    key_of = jax.random.split(jax.random.key(seed), 6)
    return {
        "queries": draw_queries(jax.random.fold_in(key_of[5], 71), 0),
        "keys": draw_keys(jax.random.fold_in(key_of[5], 71), 0),
        "values": gaussian(key_of[2], (LAT, LON, C), 1.0, 6.0, ((0, 16), (1, 32))),
        "out_weight": gaussian(key_of[3], (C, C), C ** -0.5, 0.25),
        "d_out": gaussian(key_of[4], (LAT, LON, C), 1.0, 6.0, ((0, 16), (1, 32))),
    }


def extend(field):
    wide = field.astype(jnp.float32)
    wide = jnp.concatenate([wide[:, LON - RADIUS:], wide, wide[:, :RADIUS]], axis=1)
    return jnp.pad(wide, ((RADIUS, RADIUS), (0, 0), (0, 0)))


def rounded(field):
    return lax.optimization_barrier(field.astype(jnp.bfloat16)).astype(jnp.float32)


def settle(padded):
    core = padded[RADIUS:RADIUS + LAT]
    interior = core[:, RADIUS:RADIUS + LON]
    interior = interior.at[:, LON - RADIUS:].add(core[:, :RADIUS])
    interior = interior.at[:, :RADIUS].add(core[:, LON + RADIUS:])
    return interior.astype(jnp.bfloat16)


def reference(queries, keys, values, out_weight, d_out):
    side = 2 * RADIUS + 1
    score_scale = HEAD ** -0.5
    query_full = queries.astype(jnp.float32).reshape(LAT, LON, HEADS, HEAD)
    key_pad = extend(keys)
    value_pad = extend(values)
    offsets = jnp.arange(side * side, dtype=jnp.int32)
    lat_rows = jnp.arange(LAT, dtype=jnp.int32)

    def window(padded, offset):
        start = (offset // side, offset % side, offset * 0)
        return lax.dynamic_slice(padded, start, (LAT, LON, C)).reshape(LAT, LON, HEADS, HEAD)

    def inside(offset):
        shifted = lat_rows + offset // side - RADIUS
        return ((shifted >= 0) & (shifted < LAT))[:, None, None]

    def score_step(carry, offset):
        scores = jnp.sum(query_full * window(key_pad, offset), axis=-1) * score_scale
        return carry, jnp.where(inside(offset), scores, -1e30)

    _, scores = lax.scan(score_step, jnp.float32(0.0), offsets)
    shifted_all = lat_rows[None, :] + offsets[:, None] // side - RADIUS
    valid_all = ((shifted_all >= 0) & (shifted_all < LAT))[:, :, None, None]
    peak = jnp.max(scores, axis=0)
    lifted = jnp.where(valid_all, jnp.exp(scores - peak), 0.0)
    probs = lifted / jnp.sum(lifted, axis=0)

    def attend_step(total, item):
        offset, weights = item
        return total + rounded(weights)[..., None] * window(value_pad, offset), None

    att_full, _ = lax.scan(attend_step, jnp.zeros((LAT, LON, HEADS, HEAD), jnp.float32), (offsets, probs))
    attended = att_full.reshape(TOKENS, C).astype(jnp.bfloat16)
    upstream = d_out.reshape(TOKENS, C)
    mixed_grad = jnp.dot(upstream, out_weight.T, preferred_element_type=jnp.float32).astype(jnp.bfloat16)
    d_weight = (jnp.dot(attended.T, upstream, preferred_element_type=jnp.float32) * TOKENS ** -0.5).astype(jnp.bfloat16)
    mixed_full = mixed_grad.astype(jnp.float32).reshape(LAT, LON, HEADS, HEAD)
    row_delta = jnp.sum(mixed_full * att_full, axis=-1)

    def grad_step(carry, item):
        dq_total, dk_pad, dv_pad = carry
        offset, weights = item
        key_win = window(key_pad, offset)
        value_win = window(value_pad, offset)
        d_prob = jnp.sum(mixed_full * value_win, axis=-1)
        d_score = rounded(weights * (d_prob - row_delta) * score_scale)
        soft_half = rounded(weights)
        dq_total = dq_total + d_score[..., None] * key_win
        start = (offset // side, offset % side, offset * 0)
        current = lax.dynamic_slice(dk_pad, start, (LAT, LON, C))
        dk_pad = lax.dynamic_update_slice(dk_pad, current + (d_score[..., None] * query_full).reshape(LAT, LON, C), start)
        current = lax.dynamic_slice(dv_pad, start, (LAT, LON, C))
        dv_pad = lax.dynamic_update_slice(dv_pad, current + (soft_half[..., None] * mixed_full).reshape(LAT, LON, C), start)
        return (dq_total, dk_pad, dv_pad), None

    padded_zero = jnp.zeros((LAT + 2 * RADIUS, LON + 2 * RADIUS, C), jnp.float32)
    start_carry = (jnp.zeros((LAT, LON, HEADS, HEAD), jnp.float32), padded_zero, padded_zero)
    (dq_total, dk_pad, dv_pad), _ = lax.scan(grad_step, start_carry, (offsets, probs))
    d_queries = dq_total.reshape(LAT, LON, C).astype(jnp.bfloat16)
    return d_queries, settle(dk_pad), settle(dv_pad), d_weight
```

```python
import functools
import math

import jax
import jax.numpy as jnp
from jax import lax
from jax.experimental import pallas as pl
from jax.experimental.pallas import tpu as pltpu
from jax.sharding import PartitionSpec as P

HEADS = 8
RADIUS = 6
MESH = pl.DeviceIdType.MESH
VMEM = pl.BlockSpec(memory_space=pltpu.VMEM)
N_LAT, N_LON, N_Z = 16, 32, 8
NEAR = [(u, v) for u in (-1, 0, 1) for v in (-1, 0, 1) if (u, v) != (0, 0)]
TAKE = {-1: (0, 1), 0: (0, 2), 1: (1, 1)}
LAND = {-1: (3, 1), 0: (1, 2), 1: (0, 1)}
OWNED = {-1: (0, 1), 0: (1, 2), 1: (3, 1)}


def near_device(side):
    lat, lon = lax.axis_index("lat"), lax.axis_index("lon")
    return (
        lax.rem(lat + side[0] + N_LAT, N_LAT),
        lax.rem(lon + side[1] + N_LON, N_LON),
    )


def block(ref, rows, cols):
    return ref.at[:, pl.ds(*rows), pl.ds(*cols)]


def enter(devices):
    barrier = pltpu.get_barrier_semaphore()
    for device in devices:
        pl.semaphore_signal(barrier, inc=1, device_id=device, device_id_type=MESH)
    pl.semaphore_wait(barrier, len(devices))


def halo_kernel(kv_ref, ext_ref, send_sems, recv_sems, own_sem):
    own = pltpu.make_async_copy(kv_ref, block(ext_ref, (1, 2), (1, 2)), own_sem)
    own.start()
    enter([near_device(side) for side in NEAR])
    copies = []
    for n, side in enumerate(NEAR):
        copy = pltpu.make_async_remote_copy(
            src_ref=block(kv_ref, TAKE[side[0]], TAKE[side[1]]),
            dst_ref=block(ext_ref, LAND[side[0]], LAND[side[1]]),
            send_sem=send_sems.at[n],
            recv_sem=recv_sems.at[n],
            device_id=near_device(side),
            device_id_type=MESH,
        )
        copy.start()
        copies.append(copy)
    own.wait()
    for copy in copies:
        copy.wait()


def dot_nt(a, b):
    return lax.dot_general(a, b, (((1,), (1,)), ((), ())), preferred_element_type=jnp.float32)


def attend_kernel(bias_ref, q_ref, k_ref, v_ref, w_ref, d_ref, dq_ref, dk_ref, dv_ref, pw_ref):
    upstream = d_ref[...]
    cells, width = q_ref.shape
    head = width // 2
    scale = head ** (-0.5)
    first = lax.broadcasted_iota(jnp.int32, (cells, width), 1) < head

    def pair(x):
        wide = x.astype(jnp.float32)
        both = jnp.concatenate([jnp.where(first, wide, 0.0), jnp.where(first, 0.0, wide)], axis=0)
        return both.astype(jnp.bfloat16)

    def unpair(x):
        return jnp.concatenate([x[:head, :cells], x[head:, cells:]], axis=0)

    mixed = pair(dot_nt(upstream, w_ref[...]).astype(jnp.bfloat16))
    query = pair(q_ref[...])
    key = k_ref[...]
    value = v_ref[...]
    scores = dot_nt(key, query) + bias_ref[...]
    peak = jnp.max(scores, axis=0, keepdims=True)
    lifted = jnp.exp2((scores - peak) * (scale * math.log2(math.e)))
    probs = lifted * (1.0 / jnp.sum(lifted, axis=0, keepdims=True))
    half = probs.astype(jnp.bfloat16)
    d_prob = dot_nt(value, mixed)
    delta = jnp.sum(half.astype(jnp.float32) * d_prob, axis=0, keepdims=True)
    d_score = (probs * (d_prob - delta)).astype(jnp.bfloat16)
    dk_ref[...] = (
        jnp.dot(d_score, query, preferred_element_type=jnp.float32) * scale
    ).astype(jnp.bfloat16)
    dv_ref[...] = jnp.dot(half, mixed, preferred_element_type=jnp.float32).astype(jnp.bfloat16)
    attended = unpair(jnp.dot(value.T, half, preferred_element_type=jnp.float32))
    pw_ref[...] = jnp.dot(
        attended.astype(jnp.bfloat16), upstream, preferred_element_type=jnp.float32
    ).astype(jnp.bfloat16)
    dq = unpair(jnp.dot(key.T, d_score, preferred_element_type=jnp.float32))
    dq_ref[...] = (dq.T * scale).astype(jnp.bfloat16)


def settle_kernel(
    weight_scale,
    grad_ref, part_ref,
    out_ref, weight_ref,
    side_a, side_b, corner, lat_in, q_out, q_in, z_in, gathered,
    near_send, near_recv, lat_send, lat_recv, q_send, q_recv, z_send, z_recv,
    f_send, f_recv, g_send, g_recv,
):
    lat, lon = lax.axis_index("lat"), lax.axis_index("lon")
    y_lo, z, core = lon // 16, lax.rem(lon // 2, 8), lax.rem(lon, 2)
    my_q = y_lo * 2 + core

    def lat_device(d):
        return (lax.rem(lat + d, N_LAT), lon)

    def q_of(d):
        return lax.rem(my_q + d, 4)

    def q_device(d):
        return (lat, (q_of(d) // 2) * 16 + z * 2 + lax.rem(q_of(d), 2))

    def z_device(d):
        return (lat, y_lo * 16 + lax.rem(z + d, N_Z) * 2 + core)

    def send(src, dst, send_sem, recv_sem, device):
        copy = pltpu.make_async_remote_copy(
            src_ref=src, dst_ref=dst, send_sem=send_sem, recv_sem=recv_sem,
            device_id=device, device_id_type=MESH,
        )
        copy.start()
        return copy

    enter(
        [near_device(side) for side in NEAR]
        + [lat_device(d) for d in range(1, N_LAT)]
        + [q_device(d) for d in range(1, 4)]
        + [z_device(d) for d in range(1, N_Z)]
    )
    sent = []
    lat_copies = [
        send(part_ref.at[lax.rem(lat + d, N_LAT)], lat_in.at[d], lat_send.at[d], lat_recv.at[d],
             lat_device(d))
        for d in range(1, N_LAT)
    ]
    near_copies, landed = [], []
    counts = [0, 0, 0]
    for n, side in enumerate(NEAR):
        kind = 2 if side[0] and side[1] else (0 if side[0] else 1)
        slot = (side_a, side_b, corner)[kind].at[counts[kind]]
        counts[kind] += 1
        near_copies.append(
            send(block(grad_ref, OWNED[side[0]], OWNED[side[1]]), slot, near_send.at[n],
                 near_recv.at[n], near_device(side))
        )
        landed.append((slot, TAKE[-side[0]], TAKE[-side[1]]))
    total = part_ref[lat].astype(jnp.float32)
    for d, copy in enumerate(lat_copies, 1):
        copy.wait_recv()
        total = total + lat_in[d].astype(jnp.float32)
    for j in range(4):
        q_out[j] = total[:, j * 128 : (j + 1) * 128]
    q_copies = [
        send(q_out.at[q_of(d)], q_in.at[d], q_send.at[d], q_recv.at[d], q_device(d))
        for d in range(1, 4)
    ]
    piece = q_out[my_q]
    for d, copy in enumerate(q_copies, 1):
        copy.wait_recv()
        piece = piece + q_in[d]
    z_in[z] = piece
    z_copies = [
        send(z_in.at[z], z_in.at[z], z_send.at[d], z_recv.at[d], z_device(d))
        for d in range(1, N_Z)
    ]
    for copy in near_copies:
        copy.wait_recv()
    for a in range(2):
        for b in range(2):
            owner = grad_ref[:, 1 + a, 1 + b].astype(jnp.float32)
            for slot, rows, cols in landed:
                i, j = a - rows[0], b - cols[0]
                if 0 <= i < rows[1] and 0 <= j < cols[1]:
                    owner = owner + slot[:, i, j].astype(jnp.float32)
            out_ref[:, a, b] = owner.astype(jnp.bfloat16)
    for copy in z_copies:
        copy.wait_recv()
    piece = z_in[0]
    for i in range(1, N_Z):
        piece = piece + z_in[i]
    gathered[my_q] = (piece * weight_scale).astype(jnp.bfloat16)
    f_copies = [
        send(gathered.at[my_q], gathered.at[my_q], f_send.at[d], f_recv.at[d], q_device(d))
        for d in range(1, 4)
    ]
    for copy in f_copies:
        copy.wait_recv()
    g_copies = [
        send(gathered, weight_ref.at[lat], g_send.at[d], g_recv.at[d], lat_device(d))
        for d in range(1, N_LAT)
    ]
    weight_ref[lat] = gathered[...]
    for copy in g_copies:
        copy.wait_recv()
    for copy in lat_copies + near_copies + q_copies + z_copies + f_copies + g_copies:
        copy.wait_send()


def to_quads(x):
    rows, cols, width = x.shape
    shaped = x.reshape(2, rows // 2, 2, cols // 2, width)
    return shaped.transpose(0, 2, 1, 3, 4).reshape(2, 2, rows * cols // 4, width)


def from_quads(x, rows, cols):
    width = x.shape[-1]
    shaped = x.reshape(2, 2, rows // 2, cols // 2, width)
    return shaped.transpose(0, 2, 1, 3, 4).reshape(rows, cols, width)


def window_bias(rows, cols, all_rows):
    high, wide = rows // 2, cols // 2

    def places(count):
        ids = jnp.arange(count * count * high * wide, dtype=jnp.int32)
        quad, cell = ids // (high * wide), ids % (high * wide)
        return (quad // count) * high + cell // wide, (quad % count) * wide + cell % wide

    key_row, key_col = places(4)
    key_row, key_col = key_row - high, key_col - wide
    row, col = places(2)
    grid_row = key_row + lax.axis_index("lat") * rows
    inside = (grid_row >= 0) & (grid_row < all_rows)
    near = (
        (jnp.abs(key_row[:, None] - row[None, :]) <= RADIUS)
        & (jnp.abs(key_col[:, None] - col[None, :]) <= RADIUS)
        & inside[:, None]
    )
    bias = jnp.where(near, 0.0, -1e30).astype(jnp.float32)
    return jnp.concatenate([bias, bias], axis=1)


def shards(queries, keys, values, out_weight, d_out):
    rows, cols, width = queries.shape
    all_rows = rows * N_LAT
    weight_scale = (all_rows * cols * N_LON) ** (-0.5)
    cells = rows * cols
    quad = cells // 4
    reach = 16 * quad
    bf16, f32 = jnp.bfloat16, jnp.float32
    dma = pltpu.SemaphoreType.DMA

    kv = jnp.stack([to_quads(keys), to_quads(values)])
    region = pl.pallas_call(
        halo_kernel,
        out_shape=jax.ShapeDtypeStruct((2, 4, 4, quad, width), bf16),
        in_specs=[VMEM],
        out_specs=VMEM,
        scratch_shapes=[dma((8,)), dma((8,)), dma],
        compiler_params=pltpu.CompilerParams(collective_id=0, has_side_effects=True),
        name="halo",
    )(kv)
    region = region.reshape(2, reach, width)
    query = to_quads(queries).reshape(cells, width)
    upstream = to_quads(d_out).reshape(cells, width)
    bias = window_bias(rows, cols, all_rows)
    pairs = HEADS // 2
    lanes = width // pairs
    part = pl.BlockSpec((cells, lanes), lambda h: (0, h))
    d_query, d_key, d_value, partial = pl.pallas_call(
        attend_kernel,
        grid=(pairs,),
        out_shape=(
            jax.ShapeDtypeStruct((cells, width), bf16),
            jax.ShapeDtypeStruct((reach, width), bf16),
            jax.ShapeDtypeStruct((reach, width), bf16),
            jax.ShapeDtypeStruct((width, width), bf16),
        ),
        in_specs=[
            pl.BlockSpec((reach, 2 * cells), lambda h: (0, 0)),
            part,
            pl.BlockSpec((None, reach, lanes), lambda h: (0, 0, h)),
            pl.BlockSpec((None, reach, lanes), lambda h: (1, 0, h)),
            pl.BlockSpec((lanes, width), lambda h: (h, 0)),
            pl.BlockSpec((cells, width), lambda h: (0, 0)),
        ],
        out_specs=(
            part,
            pl.BlockSpec((reach, lanes), lambda h: (0, h)),
            pl.BlockSpec((reach, lanes), lambda h: (0, h)),
            pl.BlockSpec((lanes, width), lambda h: (h, 0)),
        ),
        compiler_params=pltpu.CompilerParams(vmem_limit_bytes=48 << 20),
        name="attend",
    )(bias, query, region, region, out_weight, upstream)
    grads = jnp.stack([d_key, d_value]).reshape(2, 4, 4, quad, width)
    chunk = width // N_LAT
    settled, weight = pl.pallas_call(
        functools.partial(settle_kernel, weight_scale),
        out_shape=(
            jax.ShapeDtypeStruct((2, 2, 2, quad, width), bf16),
            jax.ShapeDtypeStruct((N_LAT, 4, chunk, width // 4), bf16),
        ),
        in_specs=[VMEM, VMEM],
        out_specs=(VMEM, VMEM),
        scratch_shapes=[
            pltpu.VMEM((2, 2, 1, 2, quad, width), bf16),
            pltpu.VMEM((2, 2, 2, 1, quad, width), bf16),
            pltpu.VMEM((4, 2, 1, 1, quad, width), bf16),
            pltpu.VMEM((N_LAT, chunk, width), bf16),
            pltpu.VMEM((4, chunk, width // 4), f32),
            pltpu.VMEM((4, chunk, width // 4), f32),
            pltpu.VMEM((N_Z, chunk, width // 4), f32),
            pltpu.VMEM((4, chunk, width // 4), bf16),
            dma((8,)), dma((8,)),
            dma((N_LAT,)), dma((N_LAT,)),
            dma((4,)), dma((4,)),
            dma((N_Z,)), dma((N_Z,)),
            dma((4,)), dma((4,)),
            dma((N_LAT,)), dma((N_LAT,)),
        ],
        compiler_params=pltpu.CompilerParams(
            collective_id=1, has_side_effects=True, vmem_limit_bytes=48 << 20
        ),
        name="settle",
    )(grads, partial.reshape(N_LAT, chunk, width))
    d_weight = weight.transpose(0, 2, 1, 3).reshape(width, width)
    return (
        from_quads(d_query.reshape(2, 2, quad, width), rows, cols),
        from_quads(settled[0], rows, cols),
        from_quads(settled[1], rows, cols),
        d_weight,
    )


def solution(mesh):
    placed = P("lat", "lon", None)
    return jax.shard_map(
        shards,
        mesh=mesh,
        in_specs=(placed, placed, placed, P(), placed),
        out_specs=(placed, placed, placed, P()),
        check_vma=False,
    )
```

```python
import functools
import math

import jax
import jax.numpy as jnp
from jax import lax
from jax.experimental import pallas as pl
from jax.experimental.pallas import tpu as pltpu
from jax.sharding import PartitionSpec as P

HEADS = 8
RADIUS = 6
MESH = pl.DeviceIdType.MESH
VMEM = pl.BlockSpec(memory_space=pltpu.VMEM)
N_LAT, N_LON, N_Z, N_X, N_Y = 16, 32, 8, 4, 8
UP, DOWN, LEFT, RIGHT = (-1, 0), (1, 0), (0, -1), (0, 1)


def near_device(side):
    lat, lon = lax.axis_index("lat"), lax.axis_index("lon")
    return (
        lax.rem(lat + side[0] + N_LAT, N_LAT),
        lax.rem(lon + side[1] + N_LON, N_LON),
    )


def enter(devices):
    barrier = pltpu.get_barrier_semaphore()
    for device in devices:
        pl.semaphore_signal(barrier, inc=1, device_id=device, device_id_type=MESH)
    pl.semaphore_wait(barrier, len(devices))


class Sender:
    def __init__(self, send_sems, recv_sems):
        self.sems = (send_sems, recv_sems)
        self.copies = []

    def __call__(self, src, dst, device):
        n = len(self.copies)
        copy = pltpu.make_async_remote_copy(
            src_ref=src, dst_ref=dst, send_sem=self.sems[0].at[n], recv_sem=self.sems[1].at[n],
            device_id=device, device_id_type=MESH,
        )
        copy.start()
        self.copies.append(copy)
        return copy

    def finish(self):
        for copy in self.copies:
            copy.wait_send()


def halo_kernel(kv_ref, ext_ref, send_sems, recv_sems, own_sem):
    own = pltpu.make_async_copy(kv_ref, ext_ref.at[:, pl.ds(1, 2), pl.ds(1, 2)], own_sem)
    own.start()
    up, down, left, right = [near_device(side) for side in (UP, DOWN, LEFT, RIGHT)]
    enter([up, down, left, right])
    send = Sender(send_sems, recv_sems)
    middle = pl.ds(1, 2)
    rows = []
    for i in range(2):
        rows.append((i, 3, send(kv_ref.at[i, 0], ext_ref.at[i, 3, middle], up)))
        rows.append((i, 0, send(kv_ref.at[i, 1], ext_ref.at[i, 0, middle], down)))
    waits = [
        send(kv_ref.at[:, :, 0], ext_ref.at[:, middle, 3], left),
        send(kv_ref.at[:, :, 1], ext_ref.at[:, middle, 0], right),
    ]
    for i, row, copy in rows:
        copy.wait_recv()
        waits.append(send(ext_ref.at[i, row, 1], ext_ref.at[i, row, 3], left))
        waits.append(send(ext_ref.at[i, row, 2], ext_ref.at[i, row, 0], right))
    own.wait()
    for copy in waits:
        copy.wait_recv()
    send.finish()


def dot_nt(a, b):
    return lax.dot_general(a, b, (((1,), (1,)), ((), ())), preferred_element_type=jnp.float32)


def attend_kernel(bias_ref, q_ref, k_ref, v_ref, w_ref, d_ref, dq_ref, dk_ref, dv_ref, pw_ref):
    upstream = d_ref[...]
    cells, width = q_ref.shape
    head = width // 2
    scale = head ** (-0.5)
    first = lax.broadcasted_iota(jnp.int32, (cells, width), 1) < head

    def pair(x):
        wide = x.astype(jnp.float32)
        both = jnp.concatenate([jnp.where(first, wide, 0.0), jnp.where(first, 0.0, wide)], axis=0)
        return both.astype(jnp.bfloat16)

    def unpair(x):
        return jnp.concatenate([x[:head, :cells], x[head:, cells:]], axis=0)

    mixed = pair(dot_nt(upstream, w_ref[...]).astype(jnp.bfloat16))
    query = pair(q_ref[...])
    key = k_ref[...]
    value = v_ref[...]
    scores = dot_nt(key, query) + bias_ref[...]
    peak = jnp.max(scores, axis=0, keepdims=True)
    lifted = jnp.exp2((scores - peak) * (scale * math.log2(math.e)))
    probs = lifted * (1.0 / jnp.sum(lifted, axis=0, keepdims=True))
    half = probs.astype(jnp.bfloat16)
    d_prob = dot_nt(value, mixed)
    delta = jnp.sum(half.astype(jnp.float32) * d_prob, axis=0, keepdims=True)
    d_score = (probs * (d_prob - delta)).astype(jnp.bfloat16)
    dk_ref[...] = (
        jnp.dot(d_score, query, preferred_element_type=jnp.float32) * scale
    ).astype(jnp.bfloat16)
    dv_ref[...] = jnp.dot(half, mixed, preferred_element_type=jnp.float32).astype(jnp.bfloat16)
    attended = unpair(jnp.dot(value.T, half, preferred_element_type=jnp.float32))
    pw_ref[...] = jnp.dot(
        attended.astype(jnp.bfloat16), upstream, preferred_element_type=jnp.float32
    ).astype(jnp.bfloat16)
    dq = unpair(jnp.dot(key.T, d_score, preferred_element_type=jnp.float32))
    dq_ref[...] = (dq.T * scale).astype(jnp.bfloat16)


def settle_kernel(
    weight_scale,
    grad_ref, part_ref,
    out_ref, weight_ref,
    from_side, row_out, from_row,
    core_in, z_out, z_in, x_out, x_in, y_in, gathered,
    send_sems, recv_sems,
):
    f32, bf16 = jnp.float32, jnp.bfloat16
    lat, lon = lax.axis_index("lat"), lax.axis_index("lon")
    x, y_hi = lat // 4, lax.rem(lat, 4)
    y_lo, z, core = lon // 16, lax.rem(lon // 2, N_Z), lax.rem(lon, 2)
    my_y = y_hi * 2 + y_lo
    sibling = (lat, y_lo * 16 + z * 2 + 1 - core)
    up, down, left, right = [near_device(side) for side in (UP, DOWN, LEFT, RIGHT)]

    def z_device(d):
        return (lat, y_lo * 16 + lax.rem(z + d, N_Z) * 2 + core)

    def x_device(d):
        return (lax.rem(x + d, N_X) * 4 + y_hi, lon)

    def y_device(d):
        place = lax.rem(my_y + d, N_Y)
        return (x * 4 + place // 2, lax.rem(place, 2) * 16 + z * 2 + core)

    enter(
        [up, down, left, right, sibling]
        + [z_device(d) for d in range(1, N_Z)]
        + [x_device(d) for d in range(1, N_X)]
        + [y_device(d) for d in range(1, N_Y)]
    )
    send = Sender(send_sems, recv_sems)
    edges = []
    for row in (0, 3):
        edges.append(send(grad_ref.at[:, row, 0], from_side.at[1, :, row], left))
        edges.append(send(grad_ref.at[:, row, 3], from_side.at[0, :, row], right))
    order = [lax.rem(z + d, N_Z) for d in range(N_Z)]
    halves = {}
    for d in (4, 3, 5, 2, 6, 1, 7, 0):
        halves[d] = send(part_ref.at[1 - core, order[d]], core_in.at[order[d]], sibling)
    middle = pl.ds(1, 2)
    sides = [
        send(grad_ref.at[:, middle, 0], from_side.at[1, :, middle], left),
        send(grad_ref.at[:, middle, 3], from_side.at[0, :, middle], right),
    ]
    rows = []
    for n, (row, device) in enumerate(((0, up), (3, down))):
        for copy in edges[2 * n : 2 * n + 2]:
            copy.wait_recv()
        for b in range(2):
            row_out[n, :, b] = (
                grad_ref[:, row, 1 + b].astype(f32) + from_side[b, :, row].astype(f32)
            ).astype(bf16)
        rows.append(send(row_out.at[n], from_row.at[1 - n], device))
    z_copies = []
    total = None
    for d in (4, 3, 5, 2, 6, 1, 7, 0):
        halves[d].wait_recv()
        chip = part_ref[core, order[d]].astype(f32) + core_in[order[d]].astype(f32)
        if d:
            z_out[d] = chip.astype(bf16)
            z_copies.append((d, send(z_out.at[d], z_in.at[d], z_device(d))))
        else:
            total = chip
    for d, copy in z_copies:
        copy.wait_recv()
        total = total + z_in[d].astype(f32)
    lanes = x_out.shape[-1]
    for j in range(N_X):
        x_out[j] = total[:, j * lanes : (j + 1) * lanes]
    x_copies = [
        send(x_out.at[lax.rem(x + d, N_X)], x_in.at[d], x_device(d)) for d in range(1, N_X)
    ]
    piece = x_out[x]
    for d, copy in enumerate(x_copies, 1):
        copy.wait_recv()
        piece = piece + x_in[d]
    y_in[my_y] = piece
    y_copies = [send(y_in.at[my_y], y_in.at[my_y], y_device(d)) for d in range(1, N_Y)]
    for copy in sides + rows:
        copy.wait_recv()
    for a in range(2):
        for b in range(2):
            out_ref[:, a, b] = (
                grad_ref[:, 1 + a, 1 + b].astype(f32)
                + from_side[b, :, 1 + a].astype(f32)
                + from_row[a, :, b].astype(f32)
            ).astype(bf16)
    for copy in y_copies:
        copy.wait_recv()
    piece = y_in[0]
    for i in range(1, N_Y):
        piece = piece + y_in[i]
    gathered[x] = (piece * weight_scale).astype(bf16)
    x_copies = [send(gathered.at[x], gathered.at[x], x_device(d)) for d in range(1, N_X)]
    for copy in x_copies:
        copy.wait_recv()
    z_copies = [
        (d, send(gathered, weight_ref.at[core, z], z_device(d))) for d in (4, 3, 5, 2, 6, 1, 7)
    ]
    last = [send(gathered, weight_ref.at[core, z], sibling)]
    weight_ref[core, z] = gathered[...]
    for d, copy in reversed(z_copies):
        copy.wait_recv()
        block = weight_ref.at[core, lax.rem(z + N_Z - d, N_Z)]
        last.append(send(block, block, sibling))
    for copy in last:
        copy.wait_recv()
    send.finish()


def to_quads(x):
    rows, cols, width = x.shape
    shaped = x.reshape(2, rows // 2, 2, cols // 2, width)
    return shaped.transpose(0, 2, 1, 3, 4).reshape(2, 2, rows * cols // 4, width)


def from_quads(x, rows, cols):
    width = x.shape[-1]
    shaped = x.reshape(2, 2, rows // 2, cols // 2, width)
    return shaped.transpose(0, 2, 1, 3, 4).reshape(rows, cols, width)


def window_bias(rows, cols, all_rows):
    high, wide = rows // 2, cols // 2

    def places(count):
        ids = jnp.arange(count * count * high * wide, dtype=jnp.int32)
        quad, cell = ids // (high * wide), ids % (high * wide)
        return (quad // count) * high + cell // wide, (quad % count) * wide + cell % wide

    key_row, key_col = places(4)
    key_row, key_col = key_row - high, key_col - wide
    row, col = places(2)
    grid_row = key_row + lax.axis_index("lat") * rows
    inside = (grid_row >= 0) & (grid_row < all_rows)
    near = (
        (jnp.abs(key_row[:, None] - row[None, :]) <= RADIUS)
        & (jnp.abs(key_col[:, None] - col[None, :]) <= RADIUS)
        & inside[:, None]
    )
    bias = jnp.where(near, 0.0, -1e30).astype(jnp.float32)
    return jnp.concatenate([bias, bias], axis=1)


def shards(queries, keys, values, out_weight, d_out):
    rows, cols, width = queries.shape
    all_rows = rows * N_LAT
    weight_scale = (all_rows * cols * N_LON) ** (-0.5)
    cells = rows * cols
    quad = cells // 4
    reach = 16 * quad
    bf16, f32 = jnp.bfloat16, jnp.float32
    dma = pltpu.SemaphoreType.DMA

    kv = jnp.stack([to_quads(keys), to_quads(values)])
    region = pl.pallas_call(
        halo_kernel,
        out_shape=jax.ShapeDtypeStruct((2, 4, 4, quad, width), bf16),
        in_specs=[VMEM],
        out_specs=VMEM,
        scratch_shapes=[dma((14,)), dma((14,)), dma],
        compiler_params=pltpu.CompilerParams(collective_id=0, has_side_effects=True),
        name="halo",
    )(kv)
    region = region.reshape(2, reach, width)
    query = to_quads(queries).reshape(cells, width)
    upstream = to_quads(d_out).reshape(cells, width)
    bias = window_bias(rows, cols, all_rows)
    pairs = HEADS // 2
    lanes = width // pairs
    part = pl.BlockSpec((cells, lanes), lambda h: (0, h))
    d_query, d_key, d_value, partial = pl.pallas_call(
        attend_kernel,
        grid=(pairs,),
        out_shape=(
            jax.ShapeDtypeStruct((cells, width), bf16),
            jax.ShapeDtypeStruct((reach, width), bf16),
            jax.ShapeDtypeStruct((reach, width), bf16),
            jax.ShapeDtypeStruct((width, width), bf16),
        ),
        in_specs=[
            pl.BlockSpec((reach, 2 * cells), lambda h: (0, 0)),
            part,
            pl.BlockSpec((None, reach, lanes), lambda h: (0, 0, h)),
            pl.BlockSpec((None, reach, lanes), lambda h: (1, 0, h)),
            pl.BlockSpec((lanes, width), lambda h: (h, 0)),
            pl.BlockSpec((cells, width), lambda h: (0, 0)),
        ],
        out_specs=(
            part,
            pl.BlockSpec((reach, lanes), lambda h: (0, h)),
            pl.BlockSpec((reach, lanes), lambda h: (0, h)),
            pl.BlockSpec((lanes, width), lambda h: (h, 0)),
        ),
        compiler_params=pltpu.CompilerParams(vmem_limit_bytes=48 << 20),
        name="attend",
    )(bias, query, region, region, out_weight, upstream)
    grads = jnp.stack([d_key, d_value]).reshape(2, 4, 4, quad, width)
    chunk = width // (2 * N_Z)
    settled, weight = pl.pallas_call(
        functools.partial(settle_kernel, weight_scale),
        out_shape=(
            jax.ShapeDtypeStruct((2, 2, 2, quad, width), bf16),
            jax.ShapeDtypeStruct((2, N_Z, N_X, chunk, lanes), bf16),
        ),
        in_specs=[VMEM, VMEM],
        out_specs=(VMEM, VMEM),
        scratch_shapes=[
            pltpu.VMEM((2, 2, 4, quad, width), bf16),
            pltpu.VMEM((2, 2, 2, quad, width), bf16),
            pltpu.VMEM((2, 2, 2, quad, width), bf16),
            pltpu.VMEM((N_Z, chunk, width), bf16),
            pltpu.VMEM((N_Z, chunk, width), bf16),
            pltpu.VMEM((N_Z, chunk, width), bf16),
            pltpu.VMEM((N_X, chunk, lanes), f32),
            pltpu.VMEM((N_X, chunk, lanes), f32),
            pltpu.VMEM((N_Y, chunk, lanes), f32),
            pltpu.VMEM((N_X, chunk, lanes), bf16),
            dma((51,)), dma((51,)),
        ],
        compiler_params=pltpu.CompilerParams(
            collective_id=1, has_side_effects=True, vmem_limit_bytes=48 << 20
        ),
        name="settle",
    )(grads, partial.reshape(2, N_Z, chunk, width))
    d_weight = weight.transpose(0, 1, 3, 2, 4).reshape(width, width)
    return (
        from_quads(d_query.reshape(2, 2, quad, width), rows, cols),
        from_quads(settled[0], rows, cols),
        from_quads(settled[1], rows, cols),
        d_weight,
    )


def solution(mesh):
    placed = P("lat", "lon", None)
    return jax.shard_map(
        shards,
        mesh=mesh,
        in_specs=(placed, placed, placed, P(), placed),
        out_specs=(placed, placed, placed, P()),
        check_vma=False,
    )
```

```python
import functools
import math

import jax
import jax.numpy as jnp
from jax import lax
from jax.experimental import pallas as pl
from jax.experimental.pallas import tpu as pltpu
from jax.sharding import PartitionSpec as P

HEADS = 8
RADIUS = 6
MESH = pl.DeviceIdType.MESH
VMEM = pl.BlockSpec(memory_space=pltpu.VMEM)
N_LAT, N_LON, N_Z, N_X, N_Y = 16, 32, 8, 4, 8
UP, DOWN, LEFT, RIGHT = (-1, 0), (1, 0), (0, -1), (0, 1)


def near_device(side):
    lat, lon = lax.axis_index("lat"), lax.axis_index("lon")
    return (
        lax.rem(lat + side[0] + N_LAT, N_LAT),
        lax.rem(lon + side[1] + N_LON, N_LON),
    )


def enter(devices):
    barrier = pltpu.get_barrier_semaphore()
    for device in devices:
        pl.semaphore_signal(barrier, inc=1, device_id=device, device_id_type=MESH)
    pl.semaphore_wait(barrier, len(devices))


class Sender:
    def __init__(self, send_sems, recv_sems):
        self.sems = (send_sems, recv_sems)
        self.copies = []

    def __call__(self, src, dst, device):
        n = len(self.copies)
        copy = pltpu.make_async_remote_copy(
            src_ref=src, dst_ref=dst, send_sem=self.sems[0].at[n], recv_sem=self.sems[1].at[n],
            device_id=device, device_id_type=MESH,
        )
        copy.start()
        self.copies.append(copy)
        return copy

    def finish(self):
        for copy in self.copies:
            copy.wait_send()


def halo_kernel(kv_ref, ext_ref, send_sems, recv_sems, own_sem):
    own = pltpu.make_async_copy(kv_ref, ext_ref.at[:, pl.ds(1, 2), pl.ds(1, 2)], own_sem)
    own.start()
    up, down, left, right = [near_device(side) for side in (UP, DOWN, LEFT, RIGHT)]
    enter([up, down, left, right])
    send = Sender(send_sems, recv_sems)
    middle = pl.ds(1, 2)
    rows = []
    for i in range(2):
        rows.append((i, 3, send(kv_ref.at[i, 0], ext_ref.at[i, 3, middle], up)))
        rows.append((i, 0, send(kv_ref.at[i, 1], ext_ref.at[i, 0, middle], down)))
    waits = [
        send(kv_ref.at[:, :, 0], ext_ref.at[:, middle, 3], left),
        send(kv_ref.at[:, :, 1], ext_ref.at[:, middle, 0], right),
    ]
    for i, row, copy in rows:
        copy.wait_recv()
        waits.append(send(ext_ref.at[i, row, 1], ext_ref.at[i, row, 3], left))
        waits.append(send(ext_ref.at[i, row, 2], ext_ref.at[i, row, 0], right))
    own.wait()
    for copy in waits:
        copy.wait_recv()
    send.finish()


def dot_nt(a, b):
    return lax.dot_general(a, b, (((1,), (1,)), ((), ())), preferred_element_type=jnp.float32)


def attend_kernel(bias_ref, q_ref, k_ref, v_ref, w_ref, d_ref, dq_ref, dk_ref, dv_ref, pw_ref):
    upstream = d_ref[...]
    cells, width = q_ref.shape
    head = width // 2
    scale = head ** (-0.5)
    first = lax.broadcasted_iota(jnp.int32, (cells, width), 1) < head

    def pair(x):
        wide = x.astype(jnp.float32)
        both = jnp.concatenate([jnp.where(first, wide, 0.0), jnp.where(first, 0.0, wide)], axis=0)
        return both.astype(jnp.bfloat16)

    def unpair(x):
        return jnp.concatenate([x[:head, :cells], x[head:, cells:]], axis=0)

    mixed = pair(dot_nt(upstream, w_ref[...]).astype(jnp.bfloat16))
    query = pair(q_ref[...])
    key = k_ref[...]
    value = v_ref[...]
    scores = dot_nt(key, query) + bias_ref[...]
    peak = jnp.max(scores, axis=0, keepdims=True)
    lifted = jnp.exp2((scores - peak) * (scale * math.log2(math.e)))
    probs = lifted * (1.0 / jnp.sum(lifted, axis=0, keepdims=True))
    half = probs.astype(jnp.bfloat16)
    d_prob = dot_nt(value, mixed)
    delta = jnp.sum(half.astype(jnp.float32) * d_prob, axis=0, keepdims=True)
    d_score = (probs * (d_prob - delta)).astype(jnp.bfloat16)
    dk_ref[...] = (
        jnp.dot(d_score, query, preferred_element_type=jnp.float32) * scale
    ).astype(jnp.bfloat16)
    dv_ref[...] = jnp.dot(half, mixed, preferred_element_type=jnp.float32).astype(jnp.bfloat16)
    attended = unpair(jnp.dot(value.T, half, preferred_element_type=jnp.float32))
    pw_ref[...] = jnp.dot(
        attended.astype(jnp.bfloat16), upstream, preferred_element_type=jnp.float32
    ).astype(jnp.bfloat16)
    dq = unpair(jnp.dot(key.T, d_score, preferred_element_type=jnp.float32))
    dq_ref[...] = (dq.T * scale).astype(jnp.bfloat16)


def settle_kernel(
    weight_scale,
    grad_ref, part_ref,
    out_ref, weight_ref,
    from_side, row_out, from_row,
    core_in, x_out, x_in, z_out, z_in, y_in, gathered,
    send_sems, recv_sems,
):
    f32, bf16 = jnp.float32, jnp.bfloat16
    lat, lon = lax.axis_index("lat"), lax.axis_index("lon")
    x, y_hi = lat // 4, lax.rem(lat, 4)
    y_lo, z, core = lon // 16, lax.rem(lon // 2, N_Z), lax.rem(lon, 2)
    my_y = y_hi * 2 + y_lo
    sibling = (lat, y_lo * 16 + z * 2 + 1 - core)
    up, down, left, right = [near_device(side) for side in (UP, DOWN, LEFT, RIGHT)]

    def z_device(d):
        return (lat, y_lo * 16 + lax.rem(z + d, N_Z) * 2 + core)

    def x_device(d):
        return (lax.rem(x + d, N_X) * 4 + y_hi, lon)

    def y_device(d):
        place = lax.rem(my_y + d, N_Y)
        return (x * 4 + place // 2, lax.rem(place, 2) * 16 + z * 2 + core)

    enter(
        [up, down, left, right, sibling]
        + [z_device(d) for d in range(1, N_Z)]
        + [x_device(d) for d in range(1, N_X)]
        + [y_device(d) for d in range(1, N_Y)]
    )
    send = Sender(send_sems, recv_sems)
    edges = []
    for row in (0, 3):
        edges.append(send(grad_ref.at[:, row, 0], from_side.at[1, :, row], left))
        edges.append(send(grad_ref.at[:, row, 3], from_side.at[0, :, row], right))
    order = [lax.rem(x + d, N_X) for d in range(N_X)]
    halves = {}
    for d in (2, 1, 3, 0):
        halves[d] = send(part_ref.at[1 - core, order[d]], core_in.at[order[d]], sibling)
    x_copies = []
    total = None
    for d in (2, 1, 3, 0):
        halves[d].wait_recv()
        chip = part_ref[core, order[d]].astype(f32) + core_in[order[d]].astype(f32)
        if d:
            x_out[d] = chip.astype(bf16)
            x_copies.append((d, send(x_out.at[d], x_in.at[d], x_device(d))))
        else:
            total = chip
    middle = pl.ds(1, 2)
    sides = [
        send(grad_ref.at[:, middle, 0], from_side.at[1, :, middle], left),
        send(grad_ref.at[:, middle, 3], from_side.at[0, :, middle], right),
    ]
    rows = []
    for n, (row, device) in enumerate(((0, up), (3, down))):
        for copy in edges[2 * n : 2 * n + 2]:
            copy.wait_recv()
        for b in range(2):
            row_out[n, :, b] = (
                grad_ref[:, row, 1 + b].astype(f32) + from_side[b, :, row].astype(f32)
            ).astype(bf16)
        rows.append(send(row_out.at[n], from_row.at[1 - n], device))
    for d, copy in x_copies:
        copy.wait_recv()
        total = total + x_in[d].astype(f32)
    high, lanes = z_out.shape[1:]
    across = total.shape[1] // lanes
    for n in range(N_Z):
        i, j = n // across, n % across
        z_out[n] = total[i * high : (i + 1) * high, j * lanes : (j + 1) * lanes].astype(bf16)
    far_first = (4, 3, 5, 2, 6, 1, 7)
    z_copies = [
        (d, send(z_out.at[lax.rem(z + d, N_Z)], z_in.at[d], z_device(d))) for d in far_first
    ]
    piece = z_out[z].astype(f32)
    for d, copy in z_copies:
        copy.wait_recv()
        piece = piece + z_in[d].astype(f32)
    y_in[my_y] = piece.astype(bf16)
    y_copies = [send(y_in.at[my_y], y_in.at[my_y], y_device(d)) for d in far_first]
    for copy in y_copies:
        copy.wait_recv()
    piece = y_in[0].astype(f32)
    for i in range(1, N_Y):
        piece = piece + y_in[i].astype(f32)
    gathered[z] = (piece * weight_scale).astype(bf16)
    z_copies = [send(gathered.at[z], gathered.at[z], z_device(d)) for d in far_first]
    for copy in z_copies:
        copy.wait_recv()
    x_copies = [(d, send(gathered, weight_ref.at[core, x], x_device(d))) for d in (2, 1, 3)]
    last = [send(gathered, weight_ref.at[core, x], sibling)]
    weight_ref[core, x] = gathered[...]
    for copy in sides + rows:
        copy.wait_recv()
    for a in range(2):
        for b in range(2):
            out_ref[:, a, b] = (
                grad_ref[:, 1 + a, 1 + b].astype(f32)
                + from_side[b, :, 1 + a].astype(f32)
                + from_row[a, :, b].astype(f32)
            ).astype(bf16)
    for d, copy in reversed(x_copies):
        copy.wait_recv()
        block = weight_ref.at[core, lax.rem(x + N_X - d, N_X)]
        last.append(send(block, block, sibling))
    for copy in last:
        copy.wait_recv()
    send.finish()


def to_quads(x):
    rows, cols, width = x.shape
    shaped = x.reshape(2, rows // 2, 2, cols // 2, width)
    return shaped.transpose(0, 2, 1, 3, 4).reshape(2, 2, rows * cols // 4, width)


def from_quads(x, rows, cols):
    width = x.shape[-1]
    shaped = x.reshape(2, 2, rows // 2, cols // 2, width)
    return shaped.transpose(0, 2, 1, 3, 4).reshape(rows, cols, width)


def window_bias(rows, cols, all_rows):
    high, wide = rows // 2, cols // 2

    def places(count):
        ids = jnp.arange(count * count * high * wide, dtype=jnp.int32)
        quad, cell = ids // (high * wide), ids % (high * wide)
        return (quad // count) * high + cell // wide, (quad % count) * wide + cell % wide

    key_row, key_col = places(4)
    key_row, key_col = key_row - high, key_col - wide
    row, col = places(2)
    grid_row = key_row + lax.axis_index("lat") * rows
    inside = (grid_row >= 0) & (grid_row < all_rows)
    near = (
        (jnp.abs(key_row[:, None] - row[None, :]) <= RADIUS)
        & (jnp.abs(key_col[:, None] - col[None, :]) <= RADIUS)
        & inside[:, None]
    )
    bias = jnp.where(near, 0.0, -1e30).astype(jnp.float32)
    return jnp.concatenate([bias, bias], axis=1)


def shards(queries, keys, values, out_weight, d_out):
    rows, cols, width = queries.shape
    all_rows = rows * N_LAT
    weight_scale = (all_rows * cols * N_LON) ** (-0.5)
    cells = rows * cols
    quad = cells // 4
    reach = 16 * quad
    bf16, f32 = jnp.bfloat16, jnp.float32
    dma = pltpu.SemaphoreType.DMA

    kv = jnp.stack([to_quads(keys), to_quads(values)])
    region = pl.pallas_call(
        halo_kernel,
        out_shape=jax.ShapeDtypeStruct((2, 4, 4, quad, width), bf16),
        in_specs=[VMEM],
        out_specs=VMEM,
        scratch_shapes=[dma((14,)), dma((14,)), dma],
        compiler_params=pltpu.CompilerParams(collective_id=0, has_side_effects=True),
        name="halo",
    )(kv)
    region = region.reshape(2, reach, width)
    query = to_quads(queries).reshape(cells, width)
    upstream = to_quads(d_out).reshape(cells, width)
    bias = window_bias(rows, cols, all_rows)
    pairs = HEADS // 2
    lanes = width // pairs
    part = pl.BlockSpec((cells, lanes), lambda h: (0, h))
    d_query, d_key, d_value, partial = pl.pallas_call(
        attend_kernel,
        grid=(pairs,),
        out_shape=(
            jax.ShapeDtypeStruct((cells, width), bf16),
            jax.ShapeDtypeStruct((reach, width), bf16),
            jax.ShapeDtypeStruct((reach, width), bf16),
            jax.ShapeDtypeStruct((width, width), bf16),
        ),
        in_specs=[
            pl.BlockSpec((reach, 2 * cells), lambda h: (0, 0)),
            part,
            pl.BlockSpec((None, reach, lanes), lambda h: (0, 0, h)),
            pl.BlockSpec((None, reach, lanes), lambda h: (1, 0, h)),
            pl.BlockSpec((lanes, width), lambda h: (h, 0)),
            pl.BlockSpec((cells, width), lambda h: (0, 0)),
        ],
        out_specs=(
            part,
            pl.BlockSpec((reach, lanes), lambda h: (0, h)),
            pl.BlockSpec((reach, lanes), lambda h: (0, h)),
            pl.BlockSpec((lanes, width), lambda h: (h, 0)),
        ),
        compiler_params=pltpu.CompilerParams(vmem_limit_bytes=48 << 20),
        name="attend",
    )(bias, query, region, region, out_weight, upstream)
    grads = jnp.stack([d_key, d_value]).reshape(2, 4, 4, quad, width)
    chunk = width // (2 * N_X)
    high = chunk * pairs // N_Z
    settled, weight = pl.pallas_call(
        functools.partial(settle_kernel, weight_scale),
        out_shape=(
            jax.ShapeDtypeStruct((2, 2, 2, quad, width), bf16),
            jax.ShapeDtypeStruct((2, N_X, N_Z, high, lanes), bf16),
        ),
        in_specs=[VMEM, VMEM],
        out_specs=(VMEM, VMEM),
        scratch_shapes=[
            pltpu.VMEM((2, 2, 4, quad, width), bf16),
            pltpu.VMEM((2, 2, 2, quad, width), bf16),
            pltpu.VMEM((2, 2, 2, quad, width), bf16),
            pltpu.VMEM((N_X, chunk, width), bf16),
            pltpu.VMEM((N_X, chunk, width), bf16),
            pltpu.VMEM((N_X, chunk, width), bf16),
            pltpu.VMEM((N_Z, high, lanes), bf16),
            pltpu.VMEM((N_Z, high, lanes), bf16),
            pltpu.VMEM((N_Y, high, lanes), bf16),
            pltpu.VMEM((N_Z, high, lanes), bf16),
            dma((43,)), dma((43,)),
        ],
        compiler_params=pltpu.CompilerParams(
            collective_id=1, has_side_effects=True, vmem_limit_bytes=48 << 20
        ),
        name="settle",
    )(grads, partial.reshape(2, N_X, chunk, width))
    d_weight = weight.reshape(-1, pairs, high, lanes).transpose(0, 2, 1, 3).reshape(width, width)
    return (
        from_quads(d_query.reshape(2, 2, quad, width), rows, cols),
        from_quads(settled[0], rows, cols),
        from_quads(settled[1], rows, cols),
        d_weight,
    )


def solution(mesh):
    placed = P("lat", "lon", None)
    return jax.shard_map(
        shards,
        mesh=mesh,
        in_specs=(placed, placed, placed, P(), placed),
        out_specs=(placed, placed, placed, P()),
        check_vma=False,
    )
```

```python
import functools
import math

import jax
import jax.numpy as jnp
from jax import lax
from jax.experimental import pallas as pl
from jax.experimental.pallas import tpu as pltpu
from jax.sharding import PartitionSpec as P

HEADS = 8
RADIUS = 6
MESH = pl.DeviceIdType.MESH
VMEM = pl.BlockSpec(memory_space=pltpu.VMEM)
N_LAT, N_LON, N_Z, N_X, N_Y = 16, 32, 8, 4, 8
UP, DOWN, LEFT, RIGHT = (-1, 0), (1, 0), (0, -1), (0, 1)


def near_device(side):
    lat, lon = lax.axis_index("lat"), lax.axis_index("lon")
    return (
        lax.rem(lat + side[0] + N_LAT, N_LAT),
        lax.rem(lon + side[1] + N_LON, N_LON),
    )


def enter(devices):
    barrier = pltpu.get_barrier_semaphore()
    for device in devices:
        pl.semaphore_signal(barrier, inc=1, device_id=device, device_id_type=MESH)
    pl.semaphore_wait(barrier, len(devices))


class Sender:
    def __init__(self, send_sems, recv_sems):
        self.sems = (send_sems, recv_sems)
        self.copies = []

    def __call__(self, src, dst, device):
        n = len(self.copies)
        copy = pltpu.make_async_remote_copy(
            src_ref=src, dst_ref=dst, send_sem=self.sems[0].at[n], recv_sem=self.sems[1].at[n],
            device_id=device, device_id_type=MESH,
        )
        copy.start()
        self.copies.append(copy)
        return copy

    def finish(self):
        for copy in self.copies:
            copy.wait_send()


def dot_nt(a, b):
    return lax.dot_general(a, b, (((1,), (1,)), ((), ())), preferred_element_type=jnp.float32)


def whole_kernel(
    weight_scale,
    bias_ref, q_ref, kv_ref, w_ref, d_ref,
    dq_ref, out_ref, weight_ref,
    ext_ref, grad_ref, part_ref, query_ref, mixed_ref, probs_ref, half_ref,
    from_side, row_out, from_row,
    core_in, x_out, x_in, z_out, z_in, y_in, gathered,
    send_sems, recv_sems, own_sem,
):
    f32, bf16 = jnp.float32, jnp.bfloat16
    lat, lon = lax.axis_index("lat"), lax.axis_index("lon")
    x, y_hi = lat // 4, lax.rem(lat, 4)
    y_lo, z, core = lon // 16, lax.rem(lon // 2, N_Z), lax.rem(lon, 2)
    my_y = y_hi * 2 + y_lo
    sibling = (lat, y_lo * 16 + z * 2 + 1 - core)
    up, down, left, right = [near_device(side) for side in (UP, DOWN, LEFT, RIGHT)]

    def z_device(d):
        return (lat, y_lo * 16 + lax.rem(z + d, N_Z) * 2 + core)

    def x_device(d):
        return (lax.rem(x + d, N_X) * 4 + y_hi, lon)

    def y_device(d):
        place = lax.rem(my_y + d, N_Y)
        return (x * 4 + place // 2, lax.rem(place, 2) * 16 + z * 2 + core)

    enter(
        [up, down, left, right, sibling]
        + [z_device(d) for d in range(1, N_Z)]
        + [x_device(d) for d in range(1, N_X)]
        + [y_device(d) for d in range(1, N_Y)]
    )
    send = Sender(send_sems, recv_sems)
    middle = pl.ds(1, 2)
    own = pltpu.make_async_copy(kv_ref, ext_ref.at[:, middle, middle], own_sem)
    own.start()
    arrivals = []
    for i in range(2):
        arrivals.append((i, 3, send(kv_ref.at[i, 0], ext_ref.at[i, 3, middle], up)))
        arrivals.append((i, 0, send(kv_ref.at[i, 1], ext_ref.at[i, 0, middle], down)))
    waits = [
        send(kv_ref.at[:, :, 0], ext_ref.at[:, middle, 3], left),
        send(kv_ref.at[:, :, 1], ext_ref.at[:, middle, 0], right),
    ]
    cells, width = q_ref.shape
    pairs = HEADS // 2
    wide = width // pairs
    head = wide // 2
    scale = head ** (-0.5)
    first = lax.broadcasted_iota(jnp.int32, (cells, wide), 1) < head

    def lanes_of(h):
        return slice(h * wide, (h + 1) * wide)

    def pair(value):
        value = value.astype(f32)
        both = jnp.concatenate([jnp.where(first, value, 0.0), jnp.where(first, 0.0, value)], axis=0)
        return both.astype(bf16)

    def unpair(value):
        return jnp.concatenate([value[:head, :cells], value[head:, cells:]], axis=0)

    def reached(i, h):
        return ext_ref[i, :, :, :, lanes_of(h)].reshape(-1, wide)

    for h in range(pairs):
        query_ref[h] = pair(q_ref[:, lanes_of(h)])
        mixed_ref[h] = pair(dot_nt(d_ref[...], w_ref[lanes_of(h), :]).astype(bf16))
    for i, row, copy in arrivals:
        copy.wait_recv()
        waits.append(send(ext_ref.at[i, row, 1], ext_ref.at[i, row, 3], left))
        waits.append(send(ext_ref.at[i, row, 2], ext_ref.at[i, row, 0], right))
    own.wait()
    for copy in waits:
        copy.wait_recv()

    def forward(h):
        scores = dot_nt(reached(0, h), query_ref[h]) + bias_ref[...]
        peak = jnp.max(scores, axis=0, keepdims=True)
        lifted = jnp.exp2((scores - peak) * (scale * math.log2(math.e)))
        probs = lifted * (1.0 / jnp.sum(lifted, axis=0, keepdims=True))
        half = probs.astype(bf16)
        probs_ref[h] = probs
        half_ref[h] = half
        attended = unpair(jnp.dot(reached(1, h).T, half, preferred_element_type=f32))
        part = jnp.dot(attended.astype(bf16), d_ref[...], preferred_element_type=f32)
        chunk = part_ref.shape[2]
        for n in range(wide // chunk):
            at = h * (wide // chunk) + n
            part_ref[at // N_X, at % N_X] = part[n * chunk : (n + 1) * chunk].astype(bf16)

    def backward(h):
        half, mixed = half_ref[h], mixed_ref[h]
        key = reached(0, h)
        d_prob = dot_nt(reached(1, h), mixed)
        delta = jnp.sum(half.astype(f32) * d_prob, axis=0, keepdims=True)
        d_score = (probs_ref[h] * (d_prob - delta)).astype(bf16)
        d_key = jnp.dot(d_score, query_ref[h], preferred_element_type=f32) * scale
        d_value = jnp.dot(half, mixed, preferred_element_type=f32)
        for i, grad in enumerate((d_key, d_value)):
            grad_ref[i, :, :, :, lanes_of(h)] = grad.astype(bf16).reshape(4, 4, -1, wide)
        dq = unpair(jnp.dot(key.T, d_score, preferred_element_type=f32))
        dq_ref[:, lanes_of(h)] = (dq.T * scale).astype(bf16)

    for h in range(pairs):
        forward(h)
    backward(0)
    order = [lax.rem(x + d, N_X) for d in range(N_X)]
    halves = {}
    for d in (2, 1, 3, 0):
        halves[d] = send(part_ref.at[1 - core, order[d]], core_in.at[order[d]], sibling)
    backward(1)
    x_copies = []
    total = None
    for d in (2, 1, 3, 0):
        halves[d].wait_recv()
        chip = part_ref[core, order[d]].astype(f32) + core_in[order[d]].astype(f32)
        if d:
            x_out[d] = chip.astype(bf16)
            x_copies.append((d, send(x_out.at[d], x_in.at[d], x_device(d))))
        else:
            total = chip
    backward(2)
    backward(3)
    for d, copy in x_copies:
        copy.wait_recv()
        total = total + x_in[d].astype(f32)
    high, lanes = z_out.shape[1:]
    across = total.shape[1] // lanes
    for n in range(N_Z):
        i, j = n // across, n % across
        z_out[n] = total[i * high : (i + 1) * high, j * lanes : (j + 1) * lanes].astype(bf16)
    far_first = (4, 3, 5, 2, 6, 1, 7)
    z_copies = [
        (d, send(z_out.at[lax.rem(z + d, N_Z)], z_in.at[d], z_device(d))) for d in far_first
    ]
    edges = []
    for row in (0, 3):
        edges.append(send(grad_ref.at[:, row, 0], from_side.at[1, :, row], left))
        edges.append(send(grad_ref.at[:, row, 3], from_side.at[0, :, row], right))
    sides = [
        send(grad_ref.at[:, middle, 0], from_side.at[1, :, middle], left),
        send(grad_ref.at[:, middle, 3], from_side.at[0, :, middle], right),
    ]
    piece = z_out[z].astype(f32)
    for d, copy in z_copies:
        copy.wait_recv()
        piece = piece + z_in[d].astype(f32)
    y_in[my_y] = piece.astype(bf16)
    y_copies = [send(y_in.at[my_y], y_in.at[my_y], y_device(d)) for d in far_first]
    rows = []
    for n, (row, device) in enumerate(((0, up), (3, down))):
        for copy in edges[2 * n : 2 * n + 2]:
            copy.wait_recv()
        for b in range(2):
            row_out[n, :, b] = (
                grad_ref[:, row, 1 + b].astype(f32) + from_side[b, :, row].astype(f32)
            ).astype(bf16)
        rows.append(send(row_out.at[n], from_row.at[1 - n], device))
    for copy in y_copies:
        copy.wait_recv()
    piece = y_in[0].astype(f32)
    for i in range(1, N_Y):
        piece = piece + y_in[i].astype(f32)
    gathered[z] = (piece * weight_scale).astype(bf16)
    z_copies = [send(gathered.at[z], gathered.at[z], z_device(d)) for d in far_first]
    for copy in z_copies:
        copy.wait_recv()
    x_copies = [(d, send(gathered, weight_ref.at[core, x], x_device(d))) for d in (2, 1, 3)]
    last = [send(gathered, weight_ref.at[core, x], sibling)]
    weight_ref[core, x] = gathered[...]
    for copy in sides + rows:
        copy.wait_recv()
    for a in range(2):
        for b in range(2):
            out_ref[:, a, b] = (
                grad_ref[:, 1 + a, 1 + b].astype(f32)
                + from_side[b, :, 1 + a].astype(f32)
                + from_row[a, :, b].astype(f32)
            ).astype(bf16)
    for d, copy in reversed(x_copies):
        copy.wait_recv()
        block = weight_ref.at[core, lax.rem(x + N_X - d, N_X)]
        last.append(send(block, block, sibling))
    for copy in last:
        copy.wait_recv()
    send.finish()


def to_quads(x):
    rows, cols, width = x.shape
    shaped = x.reshape(2, rows // 2, 2, cols // 2, width)
    return shaped.transpose(0, 2, 1, 3, 4).reshape(2, 2, rows * cols // 4, width)


def from_quads(x, rows, cols):
    width = x.shape[-1]
    shaped = x.reshape(2, 2, rows // 2, cols // 2, width)
    return shaped.transpose(0, 2, 1, 3, 4).reshape(rows, cols, width)


def window_bias(rows, cols, all_rows):
    high, wide = rows // 2, cols // 2

    def places(count):
        ids = jnp.arange(count * count * high * wide, dtype=jnp.int32)
        quad, cell = ids // (high * wide), ids % (high * wide)
        return (quad // count) * high + cell // wide, (quad % count) * wide + cell % wide

    key_row, key_col = places(4)
    key_row, key_col = key_row - high, key_col - wide
    row, col = places(2)
    grid_row = key_row + lax.axis_index("lat") * rows
    inside = (grid_row >= 0) & (grid_row < all_rows)
    near = (
        (jnp.abs(key_row[:, None] - row[None, :]) <= RADIUS)
        & (jnp.abs(key_col[:, None] - col[None, :]) <= RADIUS)
        & inside[:, None]
    )
    bias = jnp.where(near, 0.0, -1e30).astype(jnp.float32)
    return jnp.concatenate([bias, bias], axis=1)


def shards(queries, keys, values, out_weight, d_out):
    rows, cols, width = queries.shape
    all_rows = rows * N_LAT
    weight_scale = (all_rows * cols * N_LON) ** (-0.5)
    cells = rows * cols
    quad = cells // 4
    reach = 16 * quad
    bf16, f32 = jnp.bfloat16, jnp.float32
    dma = pltpu.SemaphoreType.DMA

    kv = jnp.stack([to_quads(keys), to_quads(values)])
    query = to_quads(queries).reshape(cells, width)
    upstream = to_quads(d_out).reshape(cells, width)
    bias = window_bias(rows, cols, all_rows)
    pairs = HEADS // 2
    lanes = width // pairs
    chunk = width // (2 * N_X)
    high = chunk * pairs // N_Z
    d_query, settled, weight = pl.pallas_call(
        functools.partial(whole_kernel, weight_scale),
        out_shape=(
            jax.ShapeDtypeStruct((cells, width), bf16),
            jax.ShapeDtypeStruct((2, 2, 2, quad, width), bf16),
            jax.ShapeDtypeStruct((2, N_X, N_Z, high, lanes), bf16),
        ),
        in_specs=[VMEM] * 5,
        out_specs=(VMEM, VMEM, VMEM),
        scratch_shapes=[
            pltpu.VMEM((2, 4, 4, quad, width), bf16),
            pltpu.VMEM((2, 4, 4, quad, width), bf16),
            pltpu.VMEM((2, N_X, chunk, width), bf16),
            pltpu.VMEM((pairs, 2 * cells, lanes), bf16),
            pltpu.VMEM((pairs, 2 * cells, lanes), bf16),
            pltpu.VMEM((pairs, reach, 2 * cells), f32),
            pltpu.VMEM((pairs, reach, 2 * cells), bf16),
            pltpu.VMEM((2, 2, 4, quad, width), bf16),
            pltpu.VMEM((2, 2, 2, quad, width), bf16),
            pltpu.VMEM((2, 2, 2, quad, width), bf16),
            pltpu.VMEM((N_X, chunk, width), bf16),
            pltpu.VMEM((N_X, chunk, width), bf16),
            pltpu.VMEM((N_X, chunk, width), bf16),
            pltpu.VMEM((N_Z, high, lanes), bf16),
            pltpu.VMEM((N_Z, high, lanes), bf16),
            pltpu.VMEM((N_Y, high, lanes), bf16),
            pltpu.VMEM((N_Z, high, lanes), bf16),
            dma((57,)), dma((57,)), dma,
        ],
        compiler_params=pltpu.CompilerParams(
            collective_id=0, has_side_effects=True, vmem_limit_bytes=48 << 20
        ),
        name="whole",
    )(bias, query, kv, out_weight, upstream)
    d_weight = weight.reshape(-1, pairs, high, lanes).transpose(0, 2, 1, 3).reshape(width, width)
    return (
        from_quads(d_query.reshape(2, 2, quad, width), rows, cols),
        from_quads(settled[0], rows, cols),
        from_quads(settled[1], rows, cols),
        d_weight,
    )


def solution(mesh):
    placed = P("lat", "lon", None)
    return jax.shard_map(
        shards,
        mesh=mesh,
        in_specs=(placed, placed, placed, P(), placed),
        out_specs=(placed, placed, placed, P()),
        check_vma=False,
    )
```

```python
import functools
import math

import jax
import jax.numpy as jnp
from jax import lax
from jax.experimental import pallas as pl
from jax.experimental.pallas import tpu as pltpu
from jax.sharding import PartitionSpec as P

HEADS = 8
RADIUS = 6
MESH = pl.DeviceIdType.MESH
VMEM = pl.BlockSpec(memory_space=pltpu.VMEM)
N_LAT, N_LON, N_Z, N_X, N_Y = 16, 32, 8, 4, 8
UP, DOWN, LEFT, RIGHT = (-1, 0), (1, 0), (0, -1), (0, 1)


def near_device(side):
    lat, lon = lax.axis_index("lat"), lax.axis_index("lon")
    return (
        lax.rem(lat + side[0] + N_LAT, N_LAT),
        lax.rem(lon + side[1] + N_LON, N_LON),
    )


def enter(devices):
    barrier = pltpu.get_barrier_semaphore()
    for device in devices:
        pl.semaphore_signal(barrier, inc=1, device_id=device, device_id_type=MESH)
    pl.semaphore_wait(barrier, len(devices))


class Sender:
    def __init__(self, send_sems, recv_sems):
        self.sems = (send_sems, recv_sems)
        self.copies = []

    def __call__(self, src, dst, device):
        n = len(self.copies)
        copy = pltpu.make_async_remote_copy(
            src_ref=src, dst_ref=dst, send_sem=self.sems[0].at[n], recv_sem=self.sems[1].at[n],
            device_id=device, device_id_type=MESH,
        )
        copy.start()
        self.copies.append(copy)
        return copy

    def finish(self):
        for copy in self.copies:
            copy.wait_send()


def dot_nt(a, b):
    return lax.dot_general(a, b, (((1,), (1,)), ((), ())), preferred_element_type=jnp.float32)


def quad_of(ref, a, b):
    rows, cols, _ = ref.shape
    high, wide = rows // 2, cols // 2
    strips = [
        ref[a * high + i].astype(jnp.float32)[b * wide : (b + 1) * wide] for i in range(high)
    ]
    return jnp.concatenate(strips, axis=0).astype(jnp.bfloat16)


def put_rows(ref, a, west, east, lanes):
    rows, cols, _ = ref.shape
    high, wide = rows // 2, cols // 2
    for i in range(high):
        cut = slice(i * wide, (i + 1) * wide)
        row = jnp.concatenate([west[cut], east[cut]], axis=0)
        ref[a * high + i, :, lanes] = row.astype(jnp.bfloat16)


def whole_kernel(
    weight_scale,
    bias_ref, queries_ref, keys_ref, values_ref, w_ref, d_out_ref,
    dq_ref, dk_ref, dv_ref, full_ref,
    weight_ref, q_ref, d_ref, kv_ref, ext_ref, grad_ref, part_ref, query_ref, mixed_ref, probs_ref, half_ref,
    from_side, row_out, from_row,
    core_in, x_out, x_in, z_out, z_in, y_in, gathered,
    send_sems, recv_sems, own_sem,
):
    f32, bf16 = jnp.float32, jnp.bfloat16
    lat, lon = lax.axis_index("lat"), lax.axis_index("lon")
    x, y_hi = lat // 4, lax.rem(lat, 4)
    y_lo, z, core = lon // 16, lax.rem(lon // 2, N_Z), lax.rem(lon, 2)
    my_y = y_hi * 2 + y_lo
    sibling = (lat, y_lo * 16 + z * 2 + 1 - core)
    up, down, left, right = [near_device(side) for side in (UP, DOWN, LEFT, RIGHT)]

    def z_device(d):
        return (lat, y_lo * 16 + lax.rem(z + d, N_Z) * 2 + core)

    def x_device(d):
        return (lax.rem(x + d, N_X) * 4 + y_hi, lon)

    def y_device(d):
        place = lax.rem(my_y + d, N_Y)
        return (x * 4 + place // 2, lax.rem(place, 2) * 16 + z * 2 + core)

    for i, field in enumerate((keys_ref, values_ref)):
        for a in range(2):
            for b in range(2):
                kv_ref[i, a, b] = quad_of(field, a, b)
    enter(
        [up, down, left, right, sibling]
        + [z_device(d) for d in range(1, N_Z)]
        + [x_device(d) for d in range(1, N_X)]
        + [y_device(d) for d in range(1, N_Y)]
    )
    send = Sender(send_sems, recv_sems)
    middle = pl.ds(1, 2)
    own = pltpu.make_async_copy(kv_ref, ext_ref.at[:, middle, middle], own_sem)
    own.start()
    arrivals = []
    for i in range(2):
        arrivals.append((i, 3, send(kv_ref.at[i, 0], ext_ref.at[i, 3, middle], up)))
        arrivals.append((i, 0, send(kv_ref.at[i, 1], ext_ref.at[i, 0, middle], down)))
    waits = [
        send(kv_ref.at[:, :, 0], ext_ref.at[:, middle, 3], left),
        send(kv_ref.at[:, :, 1], ext_ref.at[:, middle, 0], right),
    ]
    cells, width = q_ref.shape
    pairs = HEADS // 2
    wide = width // pairs
    head = wide // 2
    scale = head ** (-0.5)
    first = lax.broadcasted_iota(jnp.int32, (cells, wide), 1) < head

    def lanes_of(h):
        return slice(h * wide, (h + 1) * wide)

    def pair(value):
        value = value.astype(f32)
        both = jnp.concatenate([jnp.where(first, value, 0.0), jnp.where(first, 0.0, value)], axis=0)
        return both.astype(bf16)

    def unpair(value):
        return jnp.concatenate([value[:head, :cells], value[head:, cells:]], axis=0)

    def reached(i, h):
        return ext_ref[i, :, :, :, lanes_of(h)].reshape(-1, wide)

    for a in range(2):
        for b in range(2):
            at = (2 * a + b) * (cells // 4)
            q_ref[at : at + cells // 4] = quad_of(queries_ref, a, b)
            d_ref[at : at + cells // 4] = quad_of(d_out_ref, a, b)
    for h in range(pairs):
        query_ref[h] = pair(q_ref[:, lanes_of(h)])
        mixed_ref[h] = pair(dot_nt(d_ref[...], w_ref[lanes_of(h), :]).astype(bf16))
    for i, row, copy in arrivals:
        copy.wait_recv()
        waits.append(send(ext_ref.at[i, row, 1], ext_ref.at[i, row, 3], left))
        waits.append(send(ext_ref.at[i, row, 2], ext_ref.at[i, row, 0], right))
    own.wait()
    for copy in waits:
        copy.wait_recv()

    def forward(h):
        scores = dot_nt(reached(0, h), query_ref[h]) + bias_ref[...]
        peak = jnp.max(scores, axis=0, keepdims=True)
        lifted = jnp.exp2((scores - peak) * (scale * math.log2(math.e)))
        probs = lifted * (1.0 / jnp.sum(lifted, axis=0, keepdims=True))
        half = probs.astype(bf16)
        probs_ref[h] = probs
        half_ref[h] = half
        attended = unpair(jnp.dot(reached(1, h).T, half, preferred_element_type=f32))
        part = jnp.dot(attended.astype(bf16), d_ref[...], preferred_element_type=f32)
        chunk = part_ref.shape[2]
        for n in range(wide // chunk):
            at = h * (wide // chunk) + n
            part_ref[at // N_X, at % N_X] = part[n * chunk : (n + 1) * chunk].astype(bf16)

    def backward(h):
        half, mixed = half_ref[h], mixed_ref[h]
        key = reached(0, h)
        d_prob = dot_nt(reached(1, h), mixed)
        delta = jnp.sum(half.astype(f32) * d_prob, axis=0, keepdims=True)
        d_score = (probs_ref[h] * (d_prob - delta)).astype(bf16)
        d_key = jnp.dot(d_score, query_ref[h], preferred_element_type=f32) * scale
        d_value = jnp.dot(half, mixed, preferred_element_type=f32)
        for i, grad in enumerate((d_key, d_value)):
            grad_ref[i, :, :, :, lanes_of(h)] = grad.astype(bf16).reshape(4, 4, -1, wide)
        dq = unpair(jnp.dot(key.T, d_score, preferred_element_type=f32))
        dq = dq.T * scale
        size = cells // 4
        for a in range(2):
            at = 2 * a * size
            put_rows(dq_ref, a, dq[at : at + size], dq[at + size : at + 2 * size], lanes_of(h))

    for h in range(pairs):
        forward(h)
    backward(0)
    order = [lax.rem(x + d, N_X) for d in range(N_X)]
    halves = {}
    for d in (2, 1, 3, 0):
        halves[d] = send(part_ref.at[1 - core, order[d]], core_in.at[order[d]], sibling)
    backward(1)
    x_copies = []
    total = None
    for d in (2, 1, 3, 0):
        halves[d].wait_recv()
        chip = part_ref[core, order[d]].astype(f32) + core_in[order[d]].astype(f32)
        if d:
            x_out[d] = chip.astype(bf16)
            x_copies.append((d, send(x_out.at[d], x_in.at[d], x_device(d))))
        else:
            total = chip
    backward(2)
    backward(3)
    for d, copy in x_copies:
        copy.wait_recv()
        total = total + x_in[d].astype(f32)
    high, lanes = z_out.shape[1:]
    across = total.shape[1] // lanes
    for n in range(N_Z):
        i, j = n // across, n % across
        z_out[n] = total[i * high : (i + 1) * high, j * lanes : (j + 1) * lanes].astype(bf16)
    far_first = (4, 3, 5, 2, 6, 1, 7)
    z_copies = [
        (d, send(z_out.at[lax.rem(z + d, N_Z)], z_in.at[d], z_device(d))) for d in far_first
    ]
    edges = []
    for row in (0, 3):
        edges.append(send(grad_ref.at[:, row, 0], from_side.at[1, :, row], left))
        edges.append(send(grad_ref.at[:, row, 3], from_side.at[0, :, row], right))
    sides = [
        send(grad_ref.at[:, middle, 0], from_side.at[1, :, middle], left),
        send(grad_ref.at[:, middle, 3], from_side.at[0, :, middle], right),
    ]
    piece = z_out[z].astype(f32)
    for d, copy in z_copies:
        copy.wait_recv()
        piece = piece + z_in[d].astype(f32)
    y_in[my_y] = piece.astype(bf16)
    y_copies = [send(y_in.at[my_y], y_in.at[my_y], y_device(d)) for d in far_first]
    rows = []
    for n, (row, device) in enumerate(((0, up), (3, down))):
        for copy in edges[2 * n : 2 * n + 2]:
            copy.wait_recv()
        for b in range(2):
            row_out[n, :, b] = (
                grad_ref[:, row, 1 + b].astype(f32) + from_side[b, :, row].astype(f32)
            ).astype(bf16)
        rows.append(send(row_out.at[n], from_row.at[1 - n], device))
    for copy in y_copies:
        copy.wait_recv()
    piece = y_in[0].astype(f32)
    for i in range(1, N_Y):
        piece = piece + y_in[i].astype(f32)
    gathered[z] = (piece * weight_scale).astype(bf16)
    z_copies = [send(gathered.at[z], gathered.at[z], z_device(d)) for d in far_first]
    for copy in z_copies:
        copy.wait_recv()
    x_copies = [(d, send(gathered, weight_ref.at[core, x], x_device(d))) for d in (2, 1, 3)]
    last = [send(gathered, weight_ref.at[core, x], sibling)]
    weight_ref[core, x] = gathered[...]
    for copy in sides + rows:
        copy.wait_recv()
    for i, result in enumerate((dk_ref, dv_ref)):
        for a in range(2):
            sums = [
                grad_ref[i, 1 + a, 1 + b].astype(f32)
                + from_side[b, i, 1 + a].astype(f32)
                + from_row[a, i, b].astype(f32)
                for b in range(2)
            ]
            put_rows(result, a, sums[0], sums[1], slice(None))
    for d, copy in reversed(x_copies):
        copy.wait_recv()
        block = weight_ref.at[core, lax.rem(x + N_X - d, N_X)]
        last.append(send(block, block, sibling))
    for copy in last:
        copy.wait_recv()
    for at in range(2 * N_X * N_Z):
        c, k, n = at // (N_X * N_Z), at // N_Z % N_X, at % N_Z
        row = (c * N_X + k) * N_Z // across * high + n // across * high
        col = n % across * lanes
        full_ref[row : row + high, col : col + lanes] = weight_ref[c, k, n]
    send.finish()


def window_bias(rows, cols, all_rows):
    high, wide = rows // 2, cols // 2

    def places(count):
        ids = jnp.arange(count * count * high * wide, dtype=jnp.int32)
        quad, cell = ids // (high * wide), ids % (high * wide)
        return (quad // count) * high + cell // wide, (quad % count) * wide + cell % wide

    key_row, key_col = places(4)
    key_row, key_col = key_row - high, key_col - wide
    row, col = places(2)
    grid_row = key_row + lax.axis_index("lat") * rows
    inside = (grid_row >= 0) & (grid_row < all_rows)
    near = (
        (jnp.abs(key_row[:, None] - row[None, :]) <= RADIUS)
        & (jnp.abs(key_col[:, None] - col[None, :]) <= RADIUS)
        & inside[:, None]
    )
    bias = jnp.where(near, 0.0, -1e30).astype(jnp.float32)
    return jnp.concatenate([bias, bias], axis=1)


def shards(queries, keys, values, out_weight, d_out):
    rows, cols, width = queries.shape
    all_rows = rows * N_LAT
    weight_scale = (all_rows * cols * N_LON) ** (-0.5)
    cells = rows * cols
    quad = cells // 4
    reach = 16 * quad
    bf16, f32 = jnp.bfloat16, jnp.float32
    dma = pltpu.SemaphoreType.DMA

    bias = window_bias(rows, cols, all_rows)
    pairs = HEADS // 2
    lanes = width // pairs
    chunk = width // (2 * N_X)
    high = chunk * pairs // N_Z
    field = jax.ShapeDtypeStruct((rows, cols, width), bf16)
    return pl.pallas_call(
        functools.partial(whole_kernel, weight_scale),
        out_shape=(field, field, field, jax.ShapeDtypeStruct((width, width), bf16)),
        in_specs=[VMEM] * 6,
        out_specs=(VMEM,) * 4,
        scratch_shapes=[
            pltpu.VMEM((2, N_X, N_Z, high, lanes), bf16),
            pltpu.VMEM((cells, width), bf16),
            pltpu.VMEM((cells, width), bf16),
            pltpu.VMEM((2, 2, 2, quad, width), bf16),
            pltpu.VMEM((2, 4, 4, quad, width), bf16),
            pltpu.VMEM((2, 4, 4, quad, width), bf16),
            pltpu.VMEM((2, N_X, chunk, width), bf16),
            pltpu.VMEM((pairs, 2 * cells, lanes), bf16),
            pltpu.VMEM((pairs, 2 * cells, lanes), bf16),
            pltpu.VMEM((pairs, reach, 2 * cells), f32),
            pltpu.VMEM((pairs, reach, 2 * cells), bf16),
            pltpu.VMEM((2, 2, 4, quad, width), bf16),
            pltpu.VMEM((2, 2, 2, quad, width), bf16),
            pltpu.VMEM((2, 2, 2, quad, width), bf16),
            pltpu.VMEM((N_X, chunk, width), bf16),
            pltpu.VMEM((N_X, chunk, width), bf16),
            pltpu.VMEM((N_X, chunk, width), bf16),
            pltpu.VMEM((N_Z, high, lanes), bf16),
            pltpu.VMEM((N_Z, high, lanes), bf16),
            pltpu.VMEM((N_Y, high, lanes), bf16),
            pltpu.VMEM((N_Z, high, lanes), bf16),
            dma((57,)), dma((57,)), dma,
        ],
        compiler_params=pltpu.CompilerParams(
            collective_id=0, has_side_effects=True, vmem_limit_bytes=48 << 20
        ),
        name="whole",
    )(bias, queries, keys, values, out_weight, d_out)


def solution(mesh):
    placed = P("lat", "lon", None)
    return jax.shard_map(
        shards,
        mesh=mesh,
        in_specs=(placed, placed, placed, P(), placed),
        out_specs=(placed, placed, placed, P()),
        check_vma=False,
    )
```

```python
import functools
import math

import jax
import jax.numpy as jnp
from jax import lax
from jax.experimental import pallas as pl
from jax.experimental.pallas import tpu as pltpu
from jax.sharding import PartitionSpec as P

HEADS = 8
RADIUS = 6
MESH = pl.DeviceIdType.MESH
VMEM = pl.BlockSpec(memory_space=pltpu.VMEM)
N_LAT, N_LON, N_Z, N_X, N_Y = 16, 32, 8, 4, 8
UP, DOWN, LEFT, RIGHT = (-1, 0), (1, 0), (0, -1), (0, 1)


def near_device(side):
    lat, lon = lax.axis_index("lat"), lax.axis_index("lon")
    return (
        lax.rem(lat + side[0] + N_LAT, N_LAT),
        lax.rem(lon + side[1] + N_LON, N_LON),
    )


def enter(devices):
    barrier = pltpu.get_barrier_semaphore()
    for device in devices:
        pl.semaphore_signal(barrier, inc=1, device_id=device, device_id_type=MESH)
    pl.semaphore_wait(barrier, len(devices))


class Sender:
    def __init__(self, send_sems, recv_sems):
        self.sems = (send_sems, recv_sems)
        self.copies = []

    def __call__(self, src, dst, device):
        n = len(self.copies)
        copy = pltpu.make_async_remote_copy(
            src_ref=src, dst_ref=dst, send_sem=self.sems[0].at[n], recv_sem=self.sems[1].at[n],
            device_id=device, device_id_type=MESH,
        )
        copy.start()
        self.copies.append(copy)
        return copy

    def finish(self):
        for copy in self.copies:
            copy.wait_send()


def dot_nt(a, b):
    return lax.dot_general(a, b, (((1,), (1,)), ((), ())), preferred_element_type=jnp.float32)


def quad_of(ref, a, b):
    cols, rows, _ = ref.shape
    high, wide = rows // 2, cols // 2
    strips = [
        ref[b * wide + j].astype(jnp.float32)[a * high : (a + 1) * high] for j in range(wide)
    ]
    return jnp.concatenate(strips, axis=0).astype(jnp.bfloat16)


def put_rows(ref, a, west, east, lanes):
    cols, rows, _ = ref.shape
    high, wide = rows // 2, cols // 2
    for b, part in enumerate((west, east)):
        for j in range(wide):
            piece = part[j * high : (j + 1) * high].astype(jnp.bfloat16)
            ref[b * wide + j, a * high : (a + 1) * high, lanes] = piece


def whole_kernel(
    weight_scale,
    bias_ref, queries_ref, keys_ref, values_ref, w_ref, d_out_ref,
    dq_ref, dk_ref, dv_ref, full_ref,
    weight_ref, q_ref, d_ref, kv_ref, ext_ref, grad_ref, part_ref, query_ref, mixed_ref, probs_ref, half_ref,
    from_side, row_out, from_row,
    core_in, x_out, x_in, z_out, z_in, y_in, gathered,
    send_sems, recv_sems, own_sem,
):
    f32, bf16 = jnp.float32, jnp.bfloat16
    lat, lon = lax.axis_index("lat"), lax.axis_index("lon")
    x, y_hi = lat // 4, lax.rem(lat, 4)
    y_lo, z, core = lon // 16, lax.rem(lon // 2, N_Z), lax.rem(lon, 2)
    my_y = y_hi * 2 + y_lo
    sibling = (lat, y_lo * 16 + z * 2 + 1 - core)
    up, down, left, right = [near_device(side) for side in (UP, DOWN, LEFT, RIGHT)]

    def z_device(d):
        return (lat, y_lo * 16 + lax.rem(z + d, N_Z) * 2 + core)

    def x_device(d):
        return (lax.rem(x + d, N_X) * 4 + y_hi, lon)

    def y_device(d):
        place = lax.rem(my_y + d, N_Y)
        return (x * 4 + place // 2, lax.rem(place, 2) * 16 + z * 2 + core)

    for i, field in enumerate((keys_ref, values_ref)):
        for a in range(2):
            for b in range(2):
                kv_ref[i, a, b] = quad_of(field, a, b)
    enter(
        [up, down, left, right, sibling]
        + [z_device(d) for d in range(1, N_Z)]
        + [x_device(d) for d in range(1, N_X)]
        + [y_device(d) for d in range(1, N_Y)]
    )
    send = Sender(send_sems, recv_sems)
    middle = pl.ds(1, 2)
    own = pltpu.make_async_copy(kv_ref, ext_ref.at[:, middle, middle], own_sem)
    own.start()
    arrivals = []
    for i in range(2):
        arrivals.append((i, 3, send(kv_ref.at[i, 0], ext_ref.at[i, 3, middle], up)))
        arrivals.append((i, 0, send(kv_ref.at[i, 1], ext_ref.at[i, 0, middle], down)))
    waits = [
        send(kv_ref.at[:, :, 0], ext_ref.at[:, middle, 3], left),
        send(kv_ref.at[:, :, 1], ext_ref.at[:, middle, 0], right),
    ]
    cells, width = q_ref.shape
    pairs = HEADS // 2
    wide = width // pairs
    head = wide // 2
    scale = head ** (-0.5)
    first = lax.broadcasted_iota(jnp.int32, (cells, wide), 1) < head

    def lanes_of(h):
        return slice(h * wide, (h + 1) * wide)

    def pair(value):
        value = value.astype(f32)
        both = jnp.concatenate([jnp.where(first, value, 0.0), jnp.where(first, 0.0, value)], axis=0)
        return both.astype(bf16)

    def unpair(value):
        return jnp.concatenate([value[:head, :cells], value[head:, cells:]], axis=0)

    def reached(i, h):
        return ext_ref[i, :, :, :, lanes_of(h)].reshape(-1, wide)

    for a in range(2):
        for b in range(2):
            at = (2 * a + b) * (cells // 4)
            q_ref[at : at + cells // 4] = quad_of(queries_ref, a, b)
            d_ref[at : at + cells // 4] = quad_of(d_out_ref, a, b)
    for h in range(pairs):
        query_ref[h] = pair(q_ref[:, lanes_of(h)])
        mixed_ref[h] = pair(dot_nt(d_ref[...], w_ref[lanes_of(h), :]).astype(bf16))
    for i, row, copy in arrivals:
        copy.wait_recv()
        waits.append(send(ext_ref.at[i, row, 1], ext_ref.at[i, row, 3], left))
        waits.append(send(ext_ref.at[i, row, 2], ext_ref.at[i, row, 0], right))
    own.wait()
    for copy in waits:
        copy.wait_recv()

    def forward(h):
        scores = dot_nt(reached(0, h), query_ref[h]) + bias_ref[...]
        peak = jnp.max(scores, axis=0, keepdims=True)
        lifted = jnp.exp2((scores - peak) * (scale * math.log2(math.e)))
        probs = lifted * (1.0 / jnp.sum(lifted, axis=0, keepdims=True))
        half = probs.astype(bf16)
        probs_ref[h] = probs
        half_ref[h] = half
        attended = unpair(jnp.dot(reached(1, h).T, half, preferred_element_type=f32))
        part = jnp.dot(attended.astype(bf16), d_ref[...], preferred_element_type=f32)
        chunk = part_ref.shape[2]
        for n in range(wide // chunk):
            at = h * (wide // chunk) + n
            part_ref[at // N_X, at % N_X] = part[n * chunk : (n + 1) * chunk].astype(bf16)

    def backward(h):
        half, mixed = half_ref[h], mixed_ref[h]
        key = reached(0, h)
        d_prob = dot_nt(reached(1, h), mixed)
        delta = jnp.sum(half.astype(f32) * d_prob, axis=0, keepdims=True)
        d_score = (probs_ref[h] * (d_prob - delta)).astype(bf16)
        d_key = jnp.dot(d_score, query_ref[h], preferred_element_type=f32) * scale
        d_value = jnp.dot(half, mixed, preferred_element_type=f32)
        for i, grad in enumerate((d_key, d_value)):
            grad_ref[i, :, :, :, lanes_of(h)] = grad.astype(bf16).reshape(4, 4, -1, wide)
        dq = unpair(jnp.dot(key.T, d_score, preferred_element_type=f32))
        dq = dq.T * scale
        size = cells // 4
        for a in range(2):
            at = 2 * a * size
            put_rows(dq_ref, a, dq[at : at + size], dq[at + size : at + 2 * size], lanes_of(h))

    for h in range(pairs):
        forward(h)
    backward(0)
    order = [lax.rem(x + d, N_X) for d in range(N_X)]
    halves = {}
    for d in (2, 1, 3, 0):
        halves[d] = send(part_ref.at[1 - core, order[d]], core_in.at[order[d]], sibling)
    backward(1)
    x_copies = []
    total = None
    for d in (2, 1, 3, 0):
        halves[d].wait_recv()
        chip = part_ref[core, order[d]].astype(f32) + core_in[order[d]].astype(f32)
        if d:
            x_out[d] = chip.astype(bf16)
            x_copies.append((d, send(x_out.at[d], x_in.at[d], x_device(d))))
        else:
            total = chip
    backward(2)
    backward(3)
    for d, copy in x_copies:
        copy.wait_recv()
        total = total + x_in[d].astype(f32)
    high, lanes = z_out.shape[1:]
    across = total.shape[1] // lanes
    for n in range(N_Z):
        i, j = n // across, n % across
        z_out[n] = total[i * high : (i + 1) * high, j * lanes : (j + 1) * lanes].astype(bf16)
    far_first = (4, 3, 5, 2, 6, 1, 7)
    z_copies = [
        (d, send(z_out.at[lax.rem(z + d, N_Z)], z_in.at[d], z_device(d))) for d in far_first
    ]
    edges = []
    for row in (0, 3):
        edges.append(send(grad_ref.at[:, row, 0], from_side.at[1, :, row], left))
        edges.append(send(grad_ref.at[:, row, 3], from_side.at[0, :, row], right))
    sides = [
        send(grad_ref.at[:, middle, 0], from_side.at[1, :, middle], left),
        send(grad_ref.at[:, middle, 3], from_side.at[0, :, middle], right),
    ]
    piece = z_out[z].astype(f32)
    for d, copy in z_copies:
        copy.wait_recv()
        piece = piece + z_in[d].astype(f32)
    y_in[my_y] = piece.astype(bf16)
    y_copies = [send(y_in.at[my_y], y_in.at[my_y], y_device(d)) for d in far_first]
    rows = []
    for n, (row, device) in enumerate(((0, up), (3, down))):
        for copy in edges[2 * n : 2 * n + 2]:
            copy.wait_recv()
        for b in range(2):
            row_out[n, :, b] = (
                grad_ref[:, row, 1 + b].astype(f32) + from_side[b, :, row].astype(f32)
            ).astype(bf16)
        rows.append(send(row_out.at[n], from_row.at[1 - n], device))
    for copy in y_copies:
        copy.wait_recv()
    piece = y_in[0].astype(f32)
    for i in range(1, N_Y):
        piece = piece + y_in[i].astype(f32)
    gathered[z] = (piece * weight_scale).astype(bf16)
    z_copies = [send(gathered.at[z], gathered.at[z], z_device(d)) for d in far_first]
    for copy in z_copies:
        copy.wait_recv()
    x_copies = [(d, send(gathered, weight_ref.at[core, x], x_device(d))) for d in (2, 1, 3)]
    last = [send(gathered, weight_ref.at[core, x], sibling)]
    weight_ref[core, x] = gathered[...]
    for copy in sides + rows:
        copy.wait_recv()
    for i, result in enumerate((dk_ref, dv_ref)):
        for a in range(2):
            sums = [
                grad_ref[i, 1 + a, 1 + b].astype(f32)
                + from_side[b, i, 1 + a].astype(f32)
                + from_row[a, i, b].astype(f32)
                for b in range(2)
            ]
            put_rows(result, a, sums[0], sums[1], slice(None))
    for d, copy in reversed(x_copies):
        copy.wait_recv()
        block = weight_ref.at[core, lax.rem(x + N_X - d, N_X)]
        last.append(send(block, block, sibling))
    for copy in last:
        copy.wait_recv()
    for at in range(2 * N_X * N_Z):
        c, k, n = at // (N_X * N_Z), at // N_Z % N_X, at % N_Z
        row = (c * N_X + k) * N_Z // across * high + n // across * high
        col = n % across * lanes
        full_ref[row : row + high, col : col + lanes] = weight_ref[c, k, n]
    send.finish()


def window_bias(rows, cols, all_rows):
    high, wide = rows // 2, cols // 2

    def places(count):
        ids = jnp.arange(count * count * high * wide, dtype=jnp.int32)
        quad, cell = ids // (high * wide), ids % (high * wide)
        return (quad // count) * high + cell % high, (quad % count) * wide + cell // high

    key_row, key_col = places(4)
    key_row, key_col = key_row - high, key_col - wide
    row, col = places(2)
    grid_row = key_row + lax.axis_index("lat") * rows
    inside = (grid_row >= 0) & (grid_row < all_rows)
    near = (
        (jnp.abs(key_row[:, None] - row[None, :]) <= RADIUS)
        & (jnp.abs(key_col[:, None] - col[None, :]) <= RADIUS)
        & inside[:, None]
    )
    bias = jnp.where(near, 0.0, -1e30).astype(jnp.float32)
    return jnp.concatenate([bias, bias], axis=1)


def turned(field):
    return field.transpose(1, 0, 2)


def shards(queries, keys, values, out_weight, d_out):
    rows, cols, width = queries.shape
    all_rows = rows * N_LAT
    weight_scale = (all_rows * cols * N_LON) ** (-0.5)
    cells = rows * cols
    quad = cells // 4
    reach = 16 * quad
    bf16, f32 = jnp.bfloat16, jnp.float32
    dma = pltpu.SemaphoreType.DMA

    bias = window_bias(rows, cols, all_rows)
    pairs = HEADS // 2
    lanes = width // pairs
    chunk = width // (2 * N_X)
    high = chunk * pairs // N_Z
    field = jax.ShapeDtypeStruct((cols, rows, width), bf16)
    d_queries, d_keys, d_values, d_weight = pl.pallas_call(
        functools.partial(whole_kernel, weight_scale),
        out_shape=(field, field, field, jax.ShapeDtypeStruct((width, width), bf16)),
        in_specs=[VMEM] * 6,
        out_specs=(VMEM,) * 4,
        scratch_shapes=[
            pltpu.VMEM((2, N_X, N_Z, high, lanes), bf16),
            pltpu.VMEM((cells, width), bf16),
            pltpu.VMEM((cells, width), bf16),
            pltpu.VMEM((2, 2, 2, quad, width), bf16),
            pltpu.VMEM((2, 4, 4, quad, width), bf16),
            pltpu.VMEM((2, 4, 4, quad, width), bf16),
            pltpu.VMEM((2, N_X, chunk, width), bf16),
            pltpu.VMEM((pairs, 2 * cells, lanes), bf16),
            pltpu.VMEM((pairs, 2 * cells, lanes), bf16),
            pltpu.VMEM((pairs, reach, 2 * cells), f32),
            pltpu.VMEM((pairs, reach, 2 * cells), bf16),
            pltpu.VMEM((2, 2, 4, quad, width), bf16),
            pltpu.VMEM((2, 2, 2, quad, width), bf16),
            pltpu.VMEM((2, 2, 2, quad, width), bf16),
            pltpu.VMEM((N_X, chunk, width), bf16),
            pltpu.VMEM((N_X, chunk, width), bf16),
            pltpu.VMEM((N_X, chunk, width), bf16),
            pltpu.VMEM((N_Z, high, lanes), bf16),
            pltpu.VMEM((N_Z, high, lanes), bf16),
            pltpu.VMEM((N_Y, high, lanes), bf16),
            pltpu.VMEM((N_Z, high, lanes), bf16),
            dma((57,)), dma((57,)), dma,
        ],
        compiler_params=pltpu.CompilerParams(
            collective_id=0, has_side_effects=True, vmem_limit_bytes=48 << 20
        ),
        name="whole",
    )(bias, turned(queries), turned(keys), turned(values), out_weight, turned(d_out))
    return turned(d_queries), turned(d_keys), turned(d_values), d_weight


def solution(mesh):
    placed = P("lat", "lon", None)
    return jax.shard_map(
        shards,
        mesh=mesh,
        in_specs=(placed, placed, placed, P(), placed),
        out_specs=(placed, placed, placed, P()),
        check_vma=False,
    )
```
